256 devices in a mesh: row: 32 (over y, z_lo, core), col: 8 (over x, z_hi).
Axes of the slice: x: 4, y: 4, z: 8 (z_hi: 2, z_lo: 4; z = z_hi * 4 + z_lo), core: 2. Of those that a mesh axis runs over, the one named last changes fastest.
Arguments:
- weight: float32 [8192, 4096], P('row', 'col'), may hold values from -0.0625 to 0.0625
- grad: bfloat16 [8192, 4096], P('row', 'col'), may hold values from -6 to 6
- left: bfloat16 [8192, 8192], P('row', 'col'), may hold values from -0.25 to 3, as said below
- right: bfloat16 [4096, 4096], P('row', 'col'), may hold values from -0.25 to 3, as said below
- tokens: bfloat16 [4096, 8192], P('row'), may hold values from -6 to 6
Outputs:
- new_weight: float32 [8192, 4096], P('row', 'col')
- output: bfloat16 [4096, 4096], P('row', 'col')
The draws below stay inside these ranges and needn't reach their ends.
Inputs may be any that keep to these rules, and one draw needn't show every extreme that they name: left is symmetric. right is symmetric.
All inputs are finite; a program needn't handle non-finite values.
Results may differ from the reference program's by a relative error of at most 0.0056.
Values may be sent and summed in bfloat16 or wider, within the bound.
A program may use at most 64 MiB of HBM per device.

```python
import math
import jax
import jax.numpy as jnp

D = 8192
BLK = 4096
TOKENS = 4096


def symmetric_factor(key, order):
    first_key, second_key = jax.random.split(jax.random.fold_in(key, 7))
    diagonal = jax.random.uniform(first_key, (order,), jnp.float32, 0.5, 2.0)
    scale_off = 0.6 / math.sqrt(order)
    noise = jax.random.uniform(second_key, (order, order), jnp.float32, -1.0, 1.0)
    offdiag = (noise + noise.T) * scale_off
    eye_mask = jnp.eye(order, dtype=jnp.float32)
    offdiag = offdiag * (1.0 - eye_mask)
    return (offdiag + eye_mask * diagonal[:, None]).astype(jnp.bfloat16)


def draw_left(key, part):
    return symmetric_factor(key, D)


def draw_right(key, part):
    return symmetric_factor(jax.random.fold_in(key, 11), BLK)


def levels(rng, shape, shards, least, top_value):
    def one(dim, shards_of):
        draws = jax.random.uniform(jax.random.fold_in(jax.random.fold_in(rng, 6), dim), (shards_of,), jnp.float32, least / len(shards), top_value / len(shards))
        return jnp.repeat(jnp.exp(draws), shape[dim] // shards_of).reshape((-1,) + (1,) * (len(shape) - dim - 1))

    factor_of = one(*shards[0])
    for cut in shards[1:]:
        factor_of = factor_of * one(*cut)
    return factor_of


def centred(own_key, dims, scale, reach, cuts=(), held_as=jnp.bfloat16):
    array = scale * jax.random.normal(own_key, dims, jnp.float32)
    if cuts:
        array = array * levels(own_key, dims, cuts, -0.22, 0.18)
    return jnp.clip(array, -reach, reach).astype(held_as)


def setup_inputs(seed: int = 0) -> dict:
    seeds = jax.random.split(jax.random.key(seed), 6)
    return {
        "weight": centred(seeds[0], (D, BLK), D ** -0.5, 0.0625, ((0, 32), (1, 8)), jnp.float32),
        "grad": centred(seeds[1], (D, BLK), 1.0, 6.0, ((0, 32), (1, 8))),
        "left": draw_left(jax.random.fold_in(seeds[5], 71), 0),
        "right": draw_right(jax.random.fold_in(seeds[5], 71), 0),
        "tokens": centred(seeds[4], (TOKENS, D), 1.0, 6.0, ((0, 32),)),
    }


def reference(weight, grad, left, right, tokens):
    left_grad = jnp.dot(left, grad, preferred_element_type=jnp.float32).astype(jnp.bfloat16)
    precond = jnp.dot(left_grad, right, preferred_element_type=jnp.float32)
    new_weight = weight - 0.01 * precond
    narrow = new_weight.astype(jnp.bfloat16)
    output = jnp.dot(tokens, narrow, preferred_element_type=jnp.float32).astype(jnp.bfloat16)
    return new_weight, output
```

```python
import jax
import jax.numpy as jnp
from jax import lax
from jax.experimental import pallas as pl
from jax.experimental.pallas import tpu as pltpu
from jax.sharding import PartitionSpec as P

MESH = pl.DeviceIdType.MESH
BF = jnp.bfloat16
F32 = jnp.float32


def kernel(w_hbm, g_hbm, l_hbm, r_hbm, t_hbm, nw_hbm, out_hbm,
           Gp, Rp, Lp, Xp, Np, Tv, Wv, Ov, acc,
           ld, sr, sg, sl, sx, sn, rr, rg, rl, rx, rn):
    row, col = lax.axis_index("row"), lax.axis_index("col")
    y, zl, c = row // 8, (row // 2) % 4, row % 2
    x, zh = col // 2, col % 2
    yp, ym, y2 = (y + 1) % 4, (y + 3) % 4, (y + 2) % 4
    xp, xm, x2 = (x + 1) % 4, (x + 3) % 4, (x + 2) % 4

    def rid(y_, z_, c_):
        return (y_ * 4 + z_) * 2 + c_

    def dev(y_=y, z_=zl, c_=c, x_=x, h_=zh):
        return (rid(y_, z_, c_), x_ * 2 + h_)

    D_yp, D_ym = dev(y_=yp), dev(y_=ym)
    D_xp, D_xm = dev(x_=xp), dev(x_=xm)
    D_sib, D_zh = dev(c_=1 - c), dev(h_=1 - zh)
    me = row

    loads = [
        pltpu.make_async_copy(r_hbm, Rp.at[me], ld.at[0]),
        pltpu.make_async_copy(g_hbm.at[pl.ds(0, 128)], Gp.at[col, 0], ld.at[1]),
        pltpu.make_async_copy(l_hbm.at[pl.ds(0, 128)], Lp.at[col, 0], ld.at[2]),
        pltpu.make_async_copy(l_hbm.at[pl.ds(128, 128)], Lp.at[col, 1], ld.at[3]),
        pltpu.make_async_copy(t_hbm, Tv, ld.at[4]),
        pltpu.make_async_copy(w_hbm, Wv, ld.at[5]),
        pltpu.make_async_copy(g_hbm.at[pl.ds(128, 128)], Gp.at[col, 1], ld.at[6]),
    ]
    for cp in loads:
        cp.start()

    bar = pltpu.get_barrier_semaphore()
    peers = [D_yp, D_ym, D_xp, D_xm, D_sib, D_zh,
             dev(z_=(zl + 1) % 4), dev(z_=(zl + 3) % 4)]
    for p in peers:
        pl.semaphore_signal(bar, inc=1, device_id=p, device_id_type=MESH)
    pl.semaphore_wait(bar, len(peers))

    pending = []

    def send(src, sems, n, rs, d, cond=None):
        cp = pltpu.make_async_remote_copy(
            src_ref=src, dst_ref=src, send_sem=sems.at[n], recv_sem=rs,
            device_id=d, device_id_type=MESH)
        if cond is None:
            cp.start()
        else:
            pl.when(cond)(cp.start)
        pending.append((cp, cond))

    def wait_recv(ref, rs):
        pltpu.make_async_remote_copy(
            src_ref=ref, dst_ref=ref, send_sem=rs, recv_sem=rs,
            device_id=D_sib, device_id_type=MESH).wait_recv()

    zorder = [zl, zl + 1 - 2 * (zl % 2), 2 - zl // 2, 3 - 3 * (zl // 2)]

    class Rho:
        def __init__(self, buf, rows, ss, rs):
            self.buf, self.half, self.ss, self.rs, self.n = buf, rows // 2, ss, rs, 0

        def put(self, i, d, h=None, cond=None):
            k = self.n
            self.n += 1
            if h is None:
                send(self.buf.at[i], self.ss, k, self.rs.at[0, i], d, cond)
            else:
                send(self.buf.at[i, pl.ds(h * self.half, self.half)],
                     self.ss, k, self.rs.at[h, i], d, cond)

        def got(self, i, h=None):
            if h is None:
                wait_recv(self.buf.at[i], self.rs.at[0, i])
            else:
                wait_recv(self.buf.at[i, pl.ds(h * self.half, self.half)], self.rs.at[h, i])

        def own(self):
            self.put(me, dev(z_=jnp.minimum(zl + 1, 3)), cond=zl < 3)
            self.put(me, dev(z_=jnp.maximum(zl - 1, 0)), cond=zl > 0)
            self.put(me, D_yp)
            self.put(me, D_ym)
            self.put(me, D_sib)

        def Z(self, j):
            zb = zorder[j]
            i = rid(y, zb, c)
            self.got(i)
            right = zb < zl
            step = jnp.where(right, 1, -1)
            ok = jnp.where(right, zl < 3, zl > 0)
            self.put(i, dev(z_=jnp.clip(zl + step, 0, 3)), cond=ok)
            self.put(i, D_yp)
            self.put(i, D_ym)
            self.put(i, D_sib)

        def Y(self, j):
            i = rid(ym, zorder[j], c)
            self.got(i)
            self.put(i, D_yp, h=0)
            self.put(i, D_sib)
            i = rid(yp, zorder[j], c)
            self.got(i)
            self.put(i, D_ym, h=1)
            self.put(i, D_sib)

        def Y2(self, j):
            i = rid(y2, zorder[j], c)
            self.got(i, 0)
            self.got(i, 1)
            self.put(i, D_sib)

        def S(self, yy):
            for j in range(4):
                self.got(rid(yy, zorder[j], 1 - c))

    class Gamma:
        def __init__(self, buf, ss, rs):
            self.buf, self.ss, self.rs, self.n = buf, ss, rs, 0

        def put(self, i, h, d):
            k = self.n
            self.n += 1
            send(self.buf.at[i, h], self.ss, k, self.rs.at[h, i], d)

        def got(self, i, h):
            wait_recv(self.buf.at[i, h], self.rs.at[h, i])

        def own_zh(self, h):
            self.put(col, h, D_zh)

        def own_x(self):
            for h in range(2):
                self.put(col, h, D_xp if h == 0 else D_xm)
                self.put(col, h, D_xm if h == 0 else D_xp)

        def partner(self, h):
            i = x * 2 + 1 - zh
            self.got(i, h)
            self.put(i, h, D_xp)
            self.put(i, h, D_xm)

        def ring(self, b):
            hb = zh if b == 0 else 1 - zh
            self.got(xm * 2 + hb, 0)
            self.put(xm * 2 + hb, 0, D_xp)
            self.got(xp * 2 + hb, 1)
            self.put(xp * 2 + hb, 1, D_xm)

        def rest(self, b):
            hb = zh if b == 0 else 1 - zh
            self.got(xm * 2 + hb, 1)
            self.got(xp * 2 + hb, 0)
            self.got(x2 * 2 + hb, 0)
            self.got(x2 * 2 + hb, 1)

    R = Rho(Rp, 128, sr, rr)
    X = Rho(Xp, 256, sx, rx)
    N = Rho(Np, 256, sn, rn)
    G = Gamma(Gp, sg, rg)
    L = Gamma(Lp, sl, rl)

    loads[0].wait()
    R.own()
    loads[1].wait()
    loads[6].wait()
    G.own_zh(0)
    G.own_zh(1)
    G.own_x()
    loads[2].wait()
    loads[3].wait()
    L.own_x()
    L.own_zh(0)
    R.Z(1)
    R.Y(0)
    G.ring(0)
    R.Z(2)
    R.Y(1)
    R.Y2(0)
    R.Z(3)
    R.Y(2)
    R.Y2(1)
    G.partner(0)
    G.partner(1)
    R.Y(3)
    R.Y2(2)
    G.ring(1)
    L.ring(0)
    R.Y2(3)
    for yy in (y, ym, yp, y2):
        R.S(yy)
    G.rest(0)
    G.rest(1)

    acc[...] = jnp.zeros_like(acc)

    @pl.loop(0, 8)
    def _(k):
        a = Gp[k].reshape(256, 512)
        b = Rp[pl.ds(4 * k, 4)].reshape(512, 512)
        acc[...] += jnp.dot(a, b, preferred_element_type=F32)

    Xp[me] = acc[...].astype(BF)
    X.own()
    L.own_zh(1)
    L.partner(0)
    X.Z(1)
    X.Y(0)
    X.Z(2)
    X.Y(1)
    X.Y2(0)
    X.Z(3)
    X.Y(2)
    X.Y2(1)
    X.Y(3)
    X.Y2(2)
    L.partner(1)
    L.ring(1)
    L.rest(0)
    L.rest(1)

    def gather_dot(lhs, rhs, yy):
        @pl.loop(0, 2)
        def _(i):
            k = 2 * yy + i
            acc[...] += jnp.dot(lhs[k].reshape(256, 1024),
                                rhs[pl.ds(4 * k, 4)].reshape(1024, 512),
                                preferred_element_type=F32)

    acc[...] = jnp.zeros_like(acc)
    X.S(y)
    gather_dot(Lp, Xp, y)
    X.S(ym)
    gather_dot(Lp, Xp, ym)
    X.S(yp)
    gather_dot(Lp, Xp, yp)
    X.Y2(3)
    X.S(y2)
    gather_dot(Lp, Xp, y2)

    loads[4].wait()
    loads[5].wait()
    nw = Wv[...] - 0.01 * acc[...]
    Np[me] = nw.astype(BF)
    N.own()
    Wv[...] = nw
    store_nw = pltpu.make_async_copy(Wv, nw_hbm, ld.at[6])
    store_nw.start()

    def out_dot(yy):
        @pl.loop(0, 2)
        def _(i):
            k = 2 * yy + i
            acc[pl.ds(0, 128)] += jnp.dot(
                Tv[:, pl.ds(pl.multiple_of(k * 1024, 1024), 1024)],
                Np[pl.ds(4 * k, 4)].reshape(1024, 512),
                preferred_element_type=F32)

    acc[...] = jnp.zeros_like(acc)
    N.Z(1)
    N.Y(0)
    N.Z(2)
    N.Y(1)
    N.Y2(0)
    N.Z(3)
    N.Y(2)
    N.Y2(1)
    N.Y(3)
    N.Y2(2)
    N.S(y)
    out_dot(y)
    N.S(ym)
    out_dot(ym)
    N.S(yp)
    out_dot(yp)
    N.Y2(3)
    N.S(y2)
    out_dot(y2)
    Ov[...] = acc[pl.ds(0, 128)].astype(BF)
    store_out = pltpu.make_async_copy(Ov, out_hbm, ld.at[7])
    store_out.start()
    for cp, cond in pending:
        if cond is None:
            cp.wait_send()
        else:
            pl.when(cond)(cp.wait_send)
    store_nw.wait()
    store_out.wait()


def shards(weight, grad, left, right, tokens):
    any_ = pl.BlockSpec(memory_space=pl.ANY)
    dma = pltpu.SemaphoreType.DMA
    return pl.pallas_call(
        kernel,
        out_shape=(jax.ShapeDtypeStruct((256, 512), F32), jax.ShapeDtypeStruct((128, 512), BF)),
        in_specs=[any_] * 5,
        out_specs=(any_, any_),
        scratch_shapes=[
            pltpu.VMEM((8, 2, 128, 512), BF),
            pltpu.VMEM((32, 128, 512), BF),
            pltpu.VMEM((8, 2, 128, 1024), BF),
            pltpu.VMEM((32, 256, 512), BF),
            pltpu.VMEM((32, 256, 512), BF),
            pltpu.VMEM((128, 8192), BF),
            pltpu.VMEM((256, 512), F32),
            pltpu.VMEM((128, 512), BF),
            pltpu.VMEM((256, 512), F32),
            dma((8,)), dma((40,)), dma((16,)), dma((16,)), dma((40,)), dma((40,)),
            dma((2, 32)), dma((2, 8)), dma((2, 8)), dma((2, 32)), dma((2, 32)),
        ],
        compiler_params=pltpu.CompilerParams(
            collective_id=0, has_side_effects=True, vmem_limit_bytes=56 * 2**20),
    )(weight, grad, left, right, tokens)


def solution(mesh):
    return jax.shard_map(
        shards,
        mesh=mesh,
        in_specs=(
            P("row", "col"),
            P("row", "col"),
            P("row", "col"),
            P("row", "col"),
            P("row", None),
        ),
        out_specs=(P("row", "col"), P("row", "col")),
        check_vma=False,
    )
```

```python
import jax
import jax.numpy as jnp
from jax import lax
from jax.experimental import pallas as pl
from jax.experimental.pallas import tpu as pltpu
from jax.sharding import PartitionSpec as P

MESH = pl.DeviceIdType.MESH
BF = jnp.bfloat16
F32 = jnp.float32


def kernel(w_hbm, g_hbm, l_hbm, r_hbm, t_hbm, nw_hbm, out_hbm,
           Gp, Rp, Lp, Xp, Np, Tq, Wv, Ov, acc, oacc, Ob, Ib,
           ld, sr, sg, sl, sx, sn, st, so, rr, rg, rl, rx, rn, rt, ro):
    row, col = lax.axis_index("row"), lax.axis_index("col")
    y, zl, c = row // 8, (row // 2) % 4, row % 2
    x, zh = col // 2, col % 2
    yp, ym, y2 = (y + 1) % 4, (y + 3) % 4, (y + 2) % 4
    xp, xm, x2 = (x + 1) % 4, (x + 3) % 4, (x + 2) % 4

    def rid(y_, z_, c_):
        return (y_ * 4 + z_) * 2 + c_

    def dev(y_=y, z_=zl, c_=c, x_=x, h_=zh):
        return (rid(y_, z_, c_), x_ * 2 + h_)

    D_yp, D_ym = dev(y_=yp), dev(y_=ym)
    D_xp, D_xm = dev(x_=xp), dev(x_=xm)
    D_sib, D_zh = dev(c_=1 - c), dev(h_=1 - zh)
    D_zr, D_zl = dev(z_=jnp.minimum(zl + 1, 3)), dev(z_=jnp.maximum(zl - 1, 0))
    me = row

    loads = [
        pltpu.make_async_copy(r_hbm, Rp.at[me], ld.at[0]),
        pltpu.make_async_copy(g_hbm.at[pl.ds(0, 128)], Gp.at[col, 0], ld.at[1]),
        pltpu.make_async_copy(w_hbm, Wv, ld.at[5]),
        pltpu.make_async_copy(g_hbm.at[pl.ds(128, 128)], Gp.at[col, 1], ld.at[4]),
    ]
    for cp in loads:
        cp.start()
    lloads = [pltpu.make_async_copy(l_hbm.at[pl.ds(64 * q, 64)], Lp.at[col, q], ld.at[12 + q])
              for q in range(4)]
    for cp in lloads:
        cp.start()
    tcols = pl.ds(pl.multiple_of(2048 * y, 2048), 2048)
    tloads = [pltpu.make_async_copy(t_hbm.at[pl.ds(32 * q, 32), tcols], Tq.at[q, y], ld.at[8 + q])
              for q in range(4)]
    for cp in tloads:
        cp.start()

    bar = pltpu.get_barrier_semaphore()
    D_y2, D_x2 = dev(y_=y2), dev(x_=x2)
    peers = [D_yp, D_ym, D_xp, D_xm, D_sib, D_zh, D_y2, D_x2,
             dev(z_=(zl + 1) % 4), dev(z_=(zl + 3) % 4)]
    for p in peers:
        pl.semaphore_signal(bar, inc=1, device_id=p, device_id_type=MESH)
    pl.semaphore_wait(bar, len(peers))

    pending = []

    def send(src, sems, n, rs, d, cond=None):
        cp = pltpu.make_async_remote_copy(
            src_ref=src, dst_ref=src, send_sem=sems.at[n], recv_sem=rs,
            device_id=d, device_id_type=MESH)
        if cond is None:
            cp.start()
        else:
            pl.when(cond)(cp.start)
        pending.append((src, sems.at[n], cond))

    def wait_recv(ref, rs):
        pltpu.make_async_remote_copy(
            src_ref=ref, dst_ref=ref, send_sem=rs, recv_sem=rs,
            device_id=D_sib, device_id_type=MESH).wait_recv()

    zorder = [zl, 1 + zl % 2, (2 + 3 * zl) % 5, 3 - 3 * (zl // 2)]

    zinfo = []
    for zb in zorder:
        right = zb < zl
        zinfo.append((zb, jnp.where(right, zl < 3, zl > 0),
                      dev(z_=jnp.clip(zl + jnp.where(right, 1, -1), 0, 3))))

    class Rho:
        def __init__(self, buf, rows, ss, rs):
            self.buf, self.half, self.ss, self.rs = buf, rows // 2, ss, rs
            self.keys, self.done = {}, set()

        def at(self, i, h):
            return self.buf.at[i, pl.ds(h * self.half, self.half)]

        def send(self, key, src, rs, d, cond=None):
            k = self.keys.setdefault(key, len(self.keys))
            cp = pltpu.make_async_remote_copy(
                src_ref=src, dst_ref=src, send_sem=self.ss.at[k], recv_sem=rs,
                device_id=d, device_id_type=MESH)
            if cond is None:
                cp.start()
            else:
                pl.when(cond)(cp.start)
            if key not in self.done:
                self.done.add(key)
                pending.append(((self.buf, None if key[1] == "s" else self.half), (self.ss, k), cond))

        def put(self, key, i, h, d, cond=None):
            self.send((key, h), self.at(i, h), self.rs.at[h, i], d, cond)

        def sib(self, key, i):
            self.send((key, "s"), self.buf.at[i], self.rs.at[0, i], D_sib)

        def got(self, i, h):
            wait_recv(self.at(i, h), self.rs.at[h, i])

        def own(self):
            for h in range(2):
                self.put("or", me, h, D_zr, zl < 3)
                self.put("ol", me, h, D_zl, zl > 0)
                self.put("oa", me, h, D_yp if h == 0 else D_ym)
                self.put("ob", me, h, D_ym if h == 0 else D_yp)
            self.sib("o", me)

        def zpart(self, j, h):
            zb, ok, d = zinfo[j]
            i = rid(y, zb, c)
            self.got(i, h)
            self.put(("z", j), i, h, d, ok)
            self.put(("za", j), i, h, D_yp if h == 0 else D_ym)
            self.put(("zb", j), i, h, D_ym if h == 0 else D_yp)

        def zsib(self, j):
            self.sib(("z", j), rid(y, zorder[j], c))

        def Z(self, j):
            self.zpart(j, 0)
            self.zpart(j, 1)
            self.zsib(j)

        def Z12(self):
            self.zpart(1, 0)
            self.zpart(2, 0)
            self.zpart(1, 1)
            self.zpart(2, 1)
            self.zsib(1)
            self.zsib(2)

        def Y(self, j):
            a, b = rid(ym, zorder[j], c), rid(yp, zorder[j], c)
            self.got(a, 0)
            self.put(("ya", j), a, 0, D_yp)
            self.got(b, 1)
            self.put(("yb", j), b, 1, D_ym)
            self.got(a, 1)
            self.sib(("ya", j), a)
            self.got(b, 0)
            self.sib(("yb", j), b)

        def Y2(self, j):
            i = rid(y2, zorder[j], c)
            self.got(i, 0)
            self.got(i, 1)
            self.sib(("y2", j), i)

        def zy(self):
            mid = (zl + 1) // 2 == 1

            @pl.when(mid)
            def _():
                self.Z12()
                self.Y(0)
                self.Z(3)

            @pl.when(jnp.logical_not(mid))
            def _():
                self.Z(1)
                self.Y(0)
                self.Z(2)
                self.Z(3)

        def S(self, yy):
            for j in range(4):
                i = rid(yy, zorder[j], 1 - c)
                wait_recv(self.buf.at[i], self.rs.at[0, i])

    class Gamma:
        def __init__(self, buf, ss, rs, parts):
            self.buf, self.ss, self.rs, self.parts, self.n = buf, ss, rs, parts, 0

        def put(self, i, p, d):
            send(self.buf.at[i, p], self.ss, self.n, self.rs.at[p, i], d)
            self.n += 1

        def got(self, i, p):
            wait_recv(self.buf.at[i, p], self.rs.at[p, i])

        def own_zh(self, p):
            self.put(col, p, D_zh)

        def own_x(self, p):
            self.put(col, p, D_xp if p % 2 == 0 else D_xm)
            self.put(col, p, D_xm if p % 2 == 0 else D_xp)

        def partner(self, p):
            i = x * 2 + 1 - zh
            self.got(i, p)
            self.put(i, p, D_xp if p % 2 == 0 else D_xm)
            self.put(i, p, D_xm if p % 2 == 0 else D_xp)

        def ring(self, b, p):
            hb = zh if b == 0 else 1 - zh
            if p % 2 == 0:
                self.got(xm * 2 + hb, p)
                self.put(xm * 2 + hb, p, D_xp)
            else:
                self.got(xp * 2 + hb, p)
                self.put(xp * 2 + hb, p, D_xm)

        def rest(self, b, p):
            hb = zh if b == 0 else 1 - zh
            self.got((xp if p % 2 == 0 else xm) * 2 + hb, p)
            self.got(x2 * 2 + hb, p)


    class Tok:
        n = 0

        def own_y(self):
            for q, d in ((yp, D_yp), (ym, D_ym), (y2, D_y2)):
                cp = pltpu.make_async_remote_copy(
                    src_ref=t_hbm.at[pl.ds(pl.multiple_of(32 * x, 32), 32),
                                     pl.ds(pl.multiple_of(2048 * q, 2048), 2048)],
                    dst_ref=Tq.at[x, y], send_sem=st.at[self.n], recv_sem=rt.at[x, y],
                    device_id=d, device_id_type=MESH)
                cp.start()
                self.n += 1
                pending.append((cp.src_ref, cp.src_sem, None))

        def share_x(self, q):
            if True:
                wait_recv(Tq.at[x, q], rt.at[x, q])
                for d in (D_xp, D_xm, D_x2):
                    send(Tq.at[x, q], st, self.n, rt.at[x, q], d)
                    self.n += 1

        def rest(self):
            for xx in (xp, xm, x2):
                for q in (yp, ym, y2):
                    wait_recv(Tq.at[xx, q], rt.at[xx, q])

    class Nar:
        n = 0

        def put(self, i, h, d, cond=None):
            send(Np.at[i, pl.ds(128 * h, 128)], sn, self.n, rn.at[h, i], d, cond)
            self.n += 1

        def sib(self, i):
            send(Np.at[i], sn, self.n, rn.at[0, i], D_sib)
            self.n += 1

        def own(self):
            i = 2 * zl + c
            for h in range(2):
                self.put(i, h, D_zr, zl < 3)
                self.put(i, h, D_zl, zl > 0)
            self.sib(i)

        def zpart(self, j, h):
            zb, ok, d = zinfo[j]
            i = 2 * zb + c
            wait_recv(Np.at[i, pl.ds(128 * h, 128)], rn.at[h, i])
            self.put(i, h, d, ok)

        def Z12(self):
            for h in range(2):
                self.zpart(1, h)
                self.zpart(2, h)
            self.sib(2 * zorder[1] + c)
            self.sib(2 * zorder[2] + c)

        def Z3(self):
            self.zpart(3, 0)
            self.zpart(3, 1)
            self.sib(2 * zorder[3] + c)

        def S(self, j):
            i = 2 * zorder[j] + 1 - c
            wait_recv(Np.at[i], rn.at[0, i])

    R = Rho(Rp, 128, sr, rr)
    X = Rho(Xp, 256, sx, rx)
    N = Nar()
    T = Tok()
    G = Gamma(Gp, sg, rg, 2)
    L = Gamma(Lp, sl, rl, 4)


    def x_dot(k):
        acc[...] += jnp.dot(Gp[k].reshape(256, 512), Rp[pl.ds(4 * k, 4)].reshape(512, 512),
                            preferred_element_type=F32)

    def x_half(hb):
        @pl.loop(0, 4)
        def _(q):
            x_dot(2 * q + hb)

    acc[...] = jnp.zeros_like(acc)
    loads[0].wait()
    loads[1].wait()
    loads[3].wait()
    G.own_zh(0)
    R.own()
    G.own_x(0)
    G.own_x(1)
    G.partner(0)
    R.zy()
    for cp in lloads: cp.wait()
    G.own_zh(1)
    G.ring(0, 0)
    G.ring(0, 1)
    L.own_x(0)
    L.own_x(1)
    L.own_zh(0)
    L.own_zh(1)
    R.Y(1)
    R.Y2(0)
    G.ring(1, 0)
    R.Y(2)
    R.Y2(1)
    G.partner(1)
    R.Y(3)
    T.own_y()
    R.Y2(2)
    R.Y2(3)
    G.ring(1, 1)
    L.own_x(2)
    L.own_x(3)
    L.ring(0, 0)
    L.ring(0, 1)
    R.S(y)
    R.S(ym)
    R.S(yp)
    R.S(y2)
    G.rest(0, 0)
    G.rest(0, 1)
    x_half(zh)
    G.rest(1, 0)
    G.rest(1, 1)
    x_half(1 - zh)
    Xp[me] = acc[...].astype(BF)
    X.own()
    L.partner(0)
    L.ring(0, 2)
    L.ring(0, 3)
    L.partner(1)
    T.share_x(yp)
    X.zy()
    L.own_zh(2)
    L.own_zh(3)
    X.Y(1)
    L.ring(1, 0)
    L.ring(1, 1)
    X.Y2(0)
    X.Y(2)
    L.partner(2)
    X.Y2(1)
    X.Y(3)
    L.partner(3)
    L.ring(1, 2)
    X.Y2(2)
    X.Y2(3)
    L.ring(1, 3)
    T.share_x(ym)
    T.share_x(y2)
    for b in range(8): L.rest(b // 4, b % 4)

    def gather_dot(lhs, rhs, yy):
        @pl.loop(0, 2)
        def _(i):
            k = 2 * yy + i
            acc[...] += jnp.dot(lhs[k].reshape(256, 1024),
                                rhs[pl.ds(4 * k, 4)].reshape(1024, 512),
                                preferred_element_type=F32)

    acc[...] = jnp.zeros_like(acc)
    X.S(y)
    gather_dot(Lp, Xp, y)
    X.S(ym)
    gather_dot(Lp, Xp, ym)
    X.S(yp)
    gather_dot(Lp, Xp, yp)
    X.S(y2)
    gather_dot(Lp, Xp, y2)

    loads[2].wait()
    nw = Wv[...] - 0.01 * acc[...]
    Np[2 * zl + c] = nw.astype(BF)
    N.own()
    Wv[...] = nw
    store_nw = pltpu.make_async_copy(Wv, nw_hbm, ld.at[6])
    store_nw.start()

    def out_dot(j, first):
        zb = zorder[j]
        lhs = Tq[:, :, :, pl.ds(pl.multiple_of(512 * zb, 512), 512)].reshape(512, 512)
        v = jnp.dot(lhs, Np[pl.ds(2 * zb, 2)].reshape(512, 512), preferred_element_type=F32)
        if first:
            oacc[...] = v
        else:
            oacc[...] += v

    for cp in tloads:
        cp.wait()
    N.Z12()
    T.rest()
    N.S(0)
    out_dot(0, True)
    N.S(1)
    out_dot(1, False)
    N.S(2)
    out_dot(2, False)
    N.Z3()
    N.S(3)
    out_dot(3, False)
    part = oacc[...].reshape(4, 4, 32, 512)
    for q in range(4):
        Ob[q] = part[:, q].reshape(128, 512).astype(BF)
    for k, (q, d) in enumerate(((yp, D_yp), (ym, D_ym), (y2, D_y2))):
        cp = pltpu.make_async_remote_copy(
            src_ref=Ob.at[q], dst_ref=Ib.at[y], send_sem=so.at[k], recv_sem=ro.at[y],
            device_id=d, device_id_type=MESH)
        cp.start()
        pending.append((cp.src_ref, cp.src_sem, None))
    for q in range(4):
        @pl.when(q == y)
        def _(q=q):
            acc[pl.ds(0, 128)] = oacc[...].reshape(4, 4, 32, 512)[:, q].reshape(128, 512)
    for q in (yp, ym, y2):
      wait_recv(Ib.at[q], ro.at[q])
    Ov[...] = (acc[pl.ds(0, 128)] + Ib[yp].astype(F32) + Ib[ym].astype(F32)
               + Ib[y2].astype(F32)).astype(BF)
    store_out = pltpu.make_async_copy(Ov, out_hbm, ld.at[7])
    store_out.start()
    for src, sem, cond in pending:
        if isinstance(src, tuple):
            src = src[0].at[0] if src[1] is None else src[0].at[0, pl.ds(0, src[1])]
            sem = sem[0].at[sem[1]]
        cp = pltpu.make_async_remote_copy(
            src_ref=src, dst_ref=src, send_sem=sem, recv_sem=sem,
            device_id=D_sib, device_id_type=MESH)
        if cond is None:
            cp.wait_send()
        else:
            pl.when(cond)(cp.wait_send)
    store_nw.wait()
    store_out.wait()


def shards(weight, grad, left, right, tokens):
    any_ = pl.BlockSpec(memory_space=pl.ANY)
    dma = pltpu.SemaphoreType.DMA
    return pl.pallas_call(
        kernel,
        out_shape=(jax.ShapeDtypeStruct((256, 512), F32), jax.ShapeDtypeStruct((128, 512), BF)),
        in_specs=[any_] * 5,
        out_specs=(any_, any_),
        scratch_shapes=[
            pltpu.VMEM((8, 2, 128, 512), BF),
            pltpu.VMEM((32, 128, 512), BF),
            pltpu.VMEM((8, 4, 64, 1024), BF),
            pltpu.VMEM((32, 256, 512), BF),
            pltpu.VMEM((8, 256, 512), BF),
            pltpu.VMEM((4, 4, 32, 2048), BF),
            pltpu.VMEM((256, 512), F32),
            pltpu.VMEM((128, 512), BF),
            pltpu.VMEM((256, 512), F32),
            pltpu.VMEM((512, 512), F32),
            pltpu.VMEM((4, 128, 512), BF),
            pltpu.VMEM((4, 128, 512), BF),
            dma((16,)), dma((52,)), dma((16,)), dma((28,)), dma((52,)), dma((20,)), dma((12,)), dma((4,)),
            dma((2, 32)), dma((2, 8)), dma((4, 8)), dma((2, 32)), dma((2, 8)), dma((4, 4)), dma((4,)),
        ],
        compiler_params=pltpu.CompilerParams(
            collective_id=0, has_side_effects=True, vmem_limit_bytes=56 * 2**20),
    )(weight, grad, left, right, tokens)


def solution(mesh):
    return jax.shard_map(
        shards,
        mesh=mesh,
        in_specs=(
            P("row", "col"),
            P("row", "col"),
            P("row", "col"),
            P("row", "col"),
            P("row", None),
        ),
        out_specs=(P("row", "col"), P("row", "col")),
        check_vma=False,
    )
```

```python
import jax
import jax.numpy as jnp
from jax import lax
from jax.experimental import pallas as pl
from jax.experimental.pallas import tpu as pltpu
from jax.sharding import PartitionSpec as P

MESH = pl.DeviceIdType.MESH
BF = jnp.bfloat16
F32 = jnp.float32


def kernel(w_hbm, g_hbm, l_hbm, r_hbm, t_hbm, nw_hbm, out_hbm,
           Gp, Rp, Lp, Xp, Np, Tq, Wv, Ov, acc, oacc, Ob, Ib,
           ld, sr, sg, sl, sx, sn, st, so, rr, rg, rl, rx, rn, rt, ro):
    row, col = lax.axis_index("row"), lax.axis_index("col")
    y, zl, c = row // 8, (row // 2) % 4, row % 2
    x, zh = col // 2, col % 2
    yp, ym, y2 = (y + 1) % 4, (y + 3) % 4, (y + 2) % 4
    xp, xm, x2 = (x + 1) % 4, (x + 3) % 4, (x + 2) % 4

    def rid(y_, z_, c_):
        return (y_ * 4 + z_) * 2 + c_

    def dev(y_=y, z_=zl, c_=c, x_=x, h_=zh):
        return (rid(y_, z_, c_), x_ * 2 + h_)

    D_yp, D_ym = dev(y_=yp), dev(y_=ym)
    D_xp, D_xm = dev(x_=xp), dev(x_=xm)
    D_sib, D_zh = dev(c_=1 - c), dev(h_=1 - zh)
    D_zr, D_zl = dev(z_=jnp.minimum(zl + 1, 3)), dev(z_=jnp.maximum(zl - 1, 0))
    me = row

    loads = [
        pltpu.make_async_copy(r_hbm, Rp.at[me], ld.at[0]),
        pltpu.make_async_copy(g_hbm.at[pl.ds(0, 128)], Gp.at[col, 0], ld.at[1]),
        pltpu.make_async_copy(w_hbm, Wv, ld.at[5]),
        pltpu.make_async_copy(g_hbm.at[pl.ds(128, 128)], Gp.at[col, 1], ld.at[4]),
    ]
    for cp in loads:
        cp.start()
    lloads = [pltpu.make_async_copy(l_hbm.at[pl.ds(64 * q, 64)], Lp.at[col, q], ld.at[12 + q])
              for q in range(4)]
    for cp in lloads:
        cp.start()
    tcols = pl.ds(pl.multiple_of(2048 * y, 2048), 2048)
    tloads = [pltpu.make_async_copy(t_hbm.at[pl.ds(32 * q, 32), tcols], Tq.at[q, y], ld.at[8 + q])
              for q in range(4)]
    for cp in tloads:
        cp.start()

    bar = pltpu.get_barrier_semaphore()
    D_y2, D_x2 = dev(y_=y2), dev(x_=x2)
    peers = [D_yp, D_ym, D_xp, D_xm, D_sib, D_zh, D_y2, D_x2,
             dev(z_=(zl + 1) % 4), dev(z_=(zl + 3) % 4)]
    for p in peers:
        pl.semaphore_signal(bar, inc=1, device_id=p, device_id_type=MESH)
    pl.semaphore_wait(bar, len(peers))

    pending = []

    def send(src, sems, n, rs, d, cond=None):
        cp = pltpu.make_async_remote_copy(
            src_ref=src, dst_ref=src, send_sem=sems.at[n], recv_sem=rs,
            device_id=d, device_id_type=MESH)
        if cond is None:
            cp.start()
        else:
            pl.when(cond)(cp.start)
        pending.append((src, sems.at[n], cond))

    def wait_recv(ref, rs):
        pltpu.make_async_remote_copy(
            src_ref=ref, dst_ref=ref, send_sem=rs, recv_sem=rs,
            device_id=D_sib, device_id_type=MESH).wait_recv()

    zorder = [zl, 1 + zl % 2, (2 + 3 * zl) % 5, 3 - 3 * (zl // 2)]

    zinfo = []
    for zb in zorder:
        right = zb < zl
        zinfo.append((zb, jnp.where(right, zl < 3, zl > 0),
                      dev(z_=jnp.clip(zl + jnp.where(right, 1, -1), 0, 3))))

    class Rho:
        def __init__(self, buf, rows, ss, rs):
            self.buf, self.half, self.ss, self.rs = buf, rows // 2, ss, rs
            self.keys, self.done = {}, set()

        def at(self, i, h):
            return self.buf.at[i, pl.ds(h * self.half, self.half)]

        def send(self, key, src, rs, d, cond=None):
            k = self.keys.setdefault(key, len(self.keys))
            cp = pltpu.make_async_remote_copy(
                src_ref=src, dst_ref=src, send_sem=self.ss.at[k], recv_sem=rs,
                device_id=d, device_id_type=MESH)
            if cond is None:
                cp.start()
            else:
                pl.when(cond)(cp.start)
            if key not in self.done:
                self.done.add(key)
                pending.append(((self.buf, None if key[1] == "s" else self.half), (self.ss, k), cond))

        def put(self, key, i, h, d, cond=None):
            self.send((key, h), self.at(i, h), self.rs.at[h, i], d, cond)

        def sib(self, key, i):
            self.send((key, "s"), self.buf.at[i], self.rs.at[0, i], D_sib)

        def got(self, i, h):
            wait_recv(self.at(i, h), self.rs.at[h, i])

        def own(self, hs=None):
            for h in (range(2) if hs is None else (hs,)):
                self.put("or", me, h, D_zr, zl < 3)
                self.put("ol", me, h, D_zl, zl > 0)
                self.put("oa", me, h, D_yp if h == 0 else D_ym)
                self.put("ob", me, h, D_ym if h == 0 else D_yp)
            if hs != 0:
                self.sib("o", me)

        def zpart(self, j, h):
            zb, ok, d = zinfo[j]
            i = rid(y, zb, c)
            self.got(i, h)
            self.put(("z", j), i, h, d, ok)
            self.put(("za", j), i, h, D_yp if h == 0 else D_ym)
            self.put(("zb", j), i, h, D_ym if h == 0 else D_yp)

        def zsib(self, j):
            self.sib(("z", j), rid(y, zorder[j], c))

        def Z(self, j):
            self.zpart(j, 0)
            self.zpart(j, 1)
            self.zsib(j)

        def Z12(self):
            self.zpart(1, 0)
            self.zpart(2, 0)
            self.zpart(1, 1)
            self.zpart(2, 1)
            self.zsib(1)
            self.zsib(2)

        def Y(self, j):
            a, b = rid(ym, zorder[j], c), rid(yp, zorder[j], c)
            self.got(a, 0)
            self.put(("ya", j), a, 0, D_yp)
            self.got(b, 1)
            self.put(("yb", j), b, 1, D_ym)
            self.got(a, 1)
            self.sib(("ya", j), a)
            self.got(b, 0)
            self.sib(("yb", j), b)

        def Y2(self, j):
            i = rid(y2, zorder[j], c)
            self.got(i, 0)
            self.got(i, 1)
            self.sib(("y2", j), i)

        def zy(self):
            mid = (zl + 1) // 2 == 1

            @pl.when(mid)
            def _():
                self.Z12()
                self.Y(0)
                self.Z(3)

            @pl.when(jnp.logical_not(mid))
            def _():
                self.Z(1)
                self.Y(0)
                self.Z(2)
                self.Y(1)
                self.Z(3)

        def y1(self):
            @pl.when((zl + 1) // 2 == 1)
            def _():
                self.Y(1)


        def S(self, yy):
            for j in range(4):
                i = rid(yy, zorder[j], 1 - c)
                wait_recv(self.buf.at[i], self.rs.at[0, i])

    class Gamma:
        def __init__(self, buf, ss, rs, parts):
            self.buf, self.ss, self.rs, self.parts, self.n = buf, ss, rs, parts, 0

        def put(self, i, p, d):
            send(self.buf.at[i, p], self.ss, self.n, self.rs.at[p, i], d)
            self.n += 1

        def got(self, i, p):
            wait_recv(self.buf.at[i, p], self.rs.at[p, i])

        def own_zh(self, p):
            self.put(col, p, D_zh)

        def own_x(self, p):
            self.put(col, p, D_xp if p % 2 == 0 else D_xm)
            self.put(col, p, D_xm if p % 2 == 0 else D_xp)

        def partner(self, p):
            i = x * 2 + 1 - zh
            self.got(i, p)
            self.put(i, p, D_xp if p % 2 == 0 else D_xm)
            self.put(i, p, D_xm if p % 2 == 0 else D_xp)

        def ring(self, b, p):
            hb = zh if b == 0 else 1 - zh
            if p % 2 == 0:
                self.got(xm * 2 + hb, p)
                self.put(xm * 2 + hb, p, D_xp)
            else:
                self.got(xp * 2 + hb, p)
                self.put(xp * 2 + hb, p, D_xm)

        def rest(self, b, p):
            hb = zh if b == 0 else 1 - zh
            self.got((xp if p % 2 == 0 else xm) * 2 + hb, p)
            self.got(x2 * 2 + hb, p)


    class Tok:
        n = 0

        def own_y(self, r):
            if True:
                for q, d in ((yp, D_yp), (ym, D_ym), (y2, D_y2)):
                    cp = pltpu.make_async_remote_copy(
                        src_ref=t_hbm.at[pl.ds(pl.multiple_of(32 * r, 32), 32),
                                         pl.ds(pl.multiple_of(2048 * q, 2048), 2048)],
                        dst_ref=Tq.at[r, y], send_sem=st.at[self.n], recv_sem=rt.at[r, y],
                        device_id=d, device_id_type=MESH)
                    cp.start()
                    self.n += 1
                    pending.append((cp.src_ref, cp.src_sem, None))

        def share_x(self, q):
            wait_recv(Tq.at[x, q], rt.at[x, q])
            for d in (D_xp, D_xm):
                send(Tq.at[x, q], st, self.n, rt.at[x, q], d)
                self.n += 1

        def rest(self):
            for r in (xp, xm, x2):
                for q in (yp, ym, y2):
                    wait_recv(Tq.at[r, q], rt.at[r, q])

    class Nar:
        n = 0

        def put(self, i, h, d, cond=None):
            send(Np.at[i, pl.ds(128 * h, 128)], sn, self.n, rn.at[h, i], d, cond)
            self.n += 1

        def sib(self, i):
            send(Np.at[i], sn, self.n, rn.at[0, i], D_sib)
            self.n += 1

        def own(self, h):
            i = 2 * zl + c
            self.put(i, h, D_zr, zl < 3)
            self.put(i, h, D_zl, zl > 0)
            if h == 1:
                self.sib(i)

        def zpart(self, j, h):
            zb, ok, d = zinfo[j]
            i = 2 * zb + c
            wait_recv(Np.at[i, pl.ds(128 * h, 128)], rn.at[h, i])
            self.put(i, h, d, ok)

        def Z12(self):
            for h in range(2):
                self.zpart(1, h)
                self.zpart(2, h)
            self.sib(2 * zorder[1] + c)
            self.sib(2 * zorder[2] + c)

        def Z3(self):
            self.zpart(3, 0)
            self.zpart(3, 1)
            self.sib(2 * zorder[3] + c)

        def S(self, j):
            i = 2 * zorder[j] + 1 - c
            wait_recv(Np.at[i], rn.at[0, i])

    R = Rho(Rp, 128, sr, rr)
    X = Rho(Xp, 256, sx, rx)
    N = Nar()
    T = Tok()
    G = Gamma(Gp, sg, rg, 2)
    L = Gamma(Lp, sl, rl, 4)


    def x_part(h, hb):
        @pl.loop(0, 4)
        def _(q):
            k = 2 * q + hb
            acc[pl.ds(128 * h, 128)] += jnp.dot(
                Gp[k, h], Rp[pl.ds(4 * k, 4)].reshape(512, 512), preferred_element_type=F32)

    def x_done(h):
        Xp[me, pl.ds(128 * h, 128)] = acc[pl.ds(128 * h, 128)].astype(BF)
        acc[pl.ds(128 * h, 128)] = jnp.zeros((128, 512), F32)
        X.own(h)

    def p(h, yy):
        @pl.loop(0, 2)
        def _(i):
            k = 2 * yy + i
            acc[pl.ds(128 * h, 128)] += jnp.dot(
                Lp[k, pl.ds(2 * h, 2)].reshape(128, 1024),
                Xp[pl.ds(4 * k, 4)].reshape(1024, 512), preferred_element_type=F32)

    stores = []

    def finish_rows(h):
        rows = pl.ds(128 * h, 128)
        nw = Wv[rows] - 0.01 * acc[rows]
        Np[2 * zl + c, rows] = nw.astype(BF)
        N.own(h)
        Wv[rows] = nw
        cp = pltpu.make_async_copy(Wv.at[rows], nw_hbm.at[rows], ld.at[6 + h])
        cp.start()
        stores.append(cp)

    def out_dot(j, first):
        zb = zorder[j]
        lhs = Tq[:, :, :, pl.ds(pl.multiple_of(512 * zb, 512), 512)].reshape(512, 512)
        v = jnp.dot(lhs, Np[pl.ds(2 * zb, 2)].reshape(512, 512), preferred_element_type=F32)
        if first:
            oacc[...] = v
        else:
            oacc[...] += v

    acc[...] = jnp.zeros_like(acc)
    loads[0].wait()
    loads[1].wait()
    loads[3].wait()
    G.own_zh(0)
    R.own()
    G.own_x(0)
    G.own_x(1)
    T.own_y(x)
    G.partner(0)
    R.zy()
    for cp in lloads: cp.wait()
    G.own_zh(1)
    G.ring(0, 0)
    G.ring(0, 1)
    R.y1()
    R.Y2(0)
    G.ring(1, 0)
    L.own_x(0)
    L.own_x(1)
    R.Y(2)
    R.Y2(1)
    R.Y(3)
    R.Y2(2)
    G.partner(1)
    L.own_zh(0)
    L.own_zh(1)
    R.Y2(3)
    R.S(y)
    R.S(ym)
    R.S(yp)
    R.S(y2)
    G.rest(0, 0)
    G.rest(1, 0)
    G.ring(1, 1)
    x_part(0, zh)
    x_part(0, 1 - zh)
    x_done(0)
    G.rest(0, 1)
    x_part(1, zh)
    G.rest(1, 1)
    x_part(1, 1 - zh)
    x_done(1)
    L.own_x(2)
    L.own_x(3)
    L.ring(0, 0)
    L.ring(0, 1)
    L.partner(0)
    X.zy()
    L.own_zh(2)
    L.partner(1)
    L.ring(0, 2)
    L.ring(0, 3)
    X.y1()
    L.ring(1, 0)
    L.ring(1, 1)
    X.Y2(0)
    L.own_zh(3)
    L.partner(2)
    X.Y(2)
    X.Y2(1)
    X.Y(3)
    L.ring(1, 2)
    L.rest(0, 0)
    L.rest(0, 1)
    L.rest(1, 0)
    L.rest(1, 1)
    L.partner(3)
    X.S(y)
    p(0, y)
    X.S(ym)
    p(0, ym)
    X.Y2(2)
    X.S(yp)
    p(0, yp)
    X.Y2(3)
    T.own_y(x2)
    L.ring(1, 3)
    X.S(y2)
    p(0, y2)
    loads[2].wait()
    finish_rows(0)
    L.rest(0, 2)
    L.rest(0, 3)
    L.rest(1, 2)
    p(1, x)
    p(1, xp)
    L.rest(1, 3)
    T.share_x(yp)
    T.share_x(ym)
    T.share_x(y2)
    p(1, xm)
    p(1, x2)
    finish_rows(1)
    for cp in tloads: cp.wait()
    N.Z12()
    T.rest()
    N.S(0)
    out_dot(0, True)
    N.S(1)
    out_dot(1, False)
    N.S(2)
    out_dot(2, False)
    N.Z3()
    N.S(3)
    out_dot(3, False)
    part = oacc[...].reshape(4, 4, 32, 512)
    for q in range(4):
        Ob[q] = part[:, q].reshape(128, 512).astype(BF)
    for k, (q, d) in enumerate(((y2, D_y2), (yp, D_yp), (ym, D_ym))):
        cp = pltpu.make_async_remote_copy(
            src_ref=Ob.at[q], dst_ref=Ib.at[y], send_sem=so.at[k], recv_sem=ro.at[y],
            device_id=d, device_id_type=MESH)
        cp.start()
        pending.append((cp.src_ref, cp.src_sem, None))
    for q in range(4):
        @pl.when(q == y)
        def _(q=q):
            acc[pl.ds(0, 128)] = oacc[...].reshape(4, 4, 32, 512)[:, q].reshape(128, 512)
    for q in (yp, ym, y2):
      wait_recv(Ib.at[q], ro.at[q])
    Ov[...] = (acc[pl.ds(0, 128)] + Ib[yp].astype(F32) + Ib[ym].astype(F32)
              + Ib[y2].astype(F32)).astype(BF)
    store_out = pltpu.make_async_copy(Ov, out_hbm, ld.at[3])
    store_out.start()
    for src, sem, cond in pending:
        if isinstance(src, tuple):
            src = src[0].at[0] if src[1] is None else src[0].at[0, pl.ds(0, src[1])]
            sem = sem[0].at[sem[1]]
        cp = pltpu.make_async_remote_copy(
            src_ref=src, dst_ref=src, send_sem=sem, recv_sem=sem,
            device_id=D_sib, device_id_type=MESH)
        if cond is None:
            cp.wait_send()
        else:
            pl.when(cond)(cp.wait_send)
    for cp in stores:
        cp.wait()
    store_out.wait()


def place(a_hbm, b_hbm, c_hbm, d_hbm, a, b, sem):
    parts = [(a_hbm, a, c_hbm, pl.ds(64 * q, 64)) for q in range(4)] + [(b_hbm, b, d_hbm, pl.ds(0, 128))]
    takes = [pltpu.make_async_copy(s.at[r], v.at[r], sem.at[k]) for k, (s, v, o, r) in enumerate(parts)]
    puts = [pltpu.make_async_copy(v.at[r], o.at[r], sem.at[5 + k]) for k, (s, v, o, r) in enumerate(parts)]
    for cp in takes:
        cp.start()
    for t, p in zip(takes, puts):
        t.wait()
        p.start()
    for cp in puts:
        cp.wait()


def shards(weight, grad, left, right, tokens):
    any_ = pl.BlockSpec(memory_space=pl.ANY)
    dma = pltpu.SemaphoreType.DMA
    new_weight, output = pl.pallas_call(
        kernel,
        out_shape=(jax.ShapeDtypeStruct((256, 512), F32), jax.ShapeDtypeStruct((128, 512), BF)),
        in_specs=[any_] * 5,
        out_specs=(any_, any_),
        scratch_shapes=[
            pltpu.VMEM((8, 2, 128, 512), BF),
            pltpu.VMEM((32, 128, 512), BF),
            pltpu.VMEM((8, 4, 64, 1024), BF),
            pltpu.VMEM((32, 256, 512), BF),
            pltpu.VMEM((8, 256, 512), BF),
            pltpu.VMEM((4, 4, 32, 2048), BF),
            pltpu.VMEM((256, 512), F32),
            pltpu.VMEM((128, 512), BF),
            pltpu.VMEM((256, 512), F32),
            pltpu.VMEM((512, 512), F32),
            pltpu.VMEM((4, 128, 512), BF),
            pltpu.VMEM((4, 128, 512), BF),
            dma((16,)), dma((52,)), dma((16,)), dma((28,)), dma((52,)), dma((20,)), dma((12,)), dma((4,)),
            dma((2, 32)), dma((2, 8)), dma((4, 8)), dma((2, 32)), dma((2, 8)), dma((4, 4)), dma((4,)),
        ],
        compiler_params=pltpu.CompilerParams(
            collective_id=0, has_side_effects=True, vmem_limit_bytes=56 * 2**20),
    )(weight, grad, left, right, tokens)
    return pl.pallas_call(
        place,
        out_shape=(jax.ShapeDtypeStruct((256, 512), F32), jax.ShapeDtypeStruct((128, 512), BF)),
        in_specs=[any_] * 2,
        out_specs=(any_, any_),
        scratch_shapes=[pltpu.VMEM((256, 512), F32), pltpu.VMEM((128, 512), BF), dma((10,))],
    )(new_weight, output)


def solution(mesh):
    return jax.shard_map(
        shards,
        mesh=mesh,
        in_specs=(
            P("row", "col"),
            P("row", "col"),
            P("row", "col"),
            P("row", "col"),
            P("row", None),
        ),
        out_specs=(P("row", "col"), P("row", "col")),
        check_vma=False,
    )
```

```python
import jax
import jax.numpy as jnp
from jax import lax
from jax.experimental import pallas as pl
from jax.experimental.pallas import tpu as pltpu
from jax.sharding import PartitionSpec as P

MESH = pl.DeviceIdType.MESH
BF = jnp.bfloat16
F32 = jnp.float32


def kernel(w_hbm, g_hbm, l_hbm, r_hbm, t_hbm, nw_hbm, out_hbm,
           Gp, Rp, Lp, Xp, Np, Tq, Wv, Ov, acc, oacc, Ob, Ib,
           ld, sr, sg, sl, sx, sn, st, so, rr, rg, rl, rx, rn, rt, ro):
    row, col = lax.axis_index("row"), lax.axis_index("col")
    y, zl, c = row // 8, (row // 2) % 4, row % 2
    x, zh = col // 2, col % 2
    yp, ym, y2 = (y + 1) % 4, (y + 3) % 4, (y + 2) % 4
    xp, xm, x2 = (x + 1) % 4, (x + 3) % 4, (x + 2) % 4

    def rid(y_, z_, c_):
        return (y_ * 4 + z_) * 2 + c_

    def dev(y_=y, z_=zl, c_=c, x_=x, h_=zh):
        return (rid(y_, z_, c_), x_ * 2 + h_)

    D_yp, D_ym = dev(y_=yp), dev(y_=ym)
    D_xp, D_xm = dev(x_=xp), dev(x_=xm)
    D_sib, D_zh = dev(c_=1 - c), dev(h_=1 - zh)
    D_zr, D_zl = dev(z_=jnp.minimum(zl + 1, 3)), dev(z_=jnp.maximum(zl - 1, 0))
    me = row

    loads = [
        pltpu.make_async_copy(r_hbm, Rp.at[me], ld.at[0]),
        pltpu.make_async_copy(g_hbm.at[pl.ds(0, 128)], Gp.at[col, 0], ld.at[1]),
        pltpu.make_async_copy(w_hbm, Wv, ld.at[5]),
        pltpu.make_async_copy(g_hbm.at[pl.ds(128, 128)], Gp.at[col, 1], ld.at[4]),
    ]
    for cp in loads:
        cp.start()
    lloads = [pltpu.make_async_copy(l_hbm.at[pl.ds(64 * q, 64)], Lp.at[col, q], ld.at[12 + q])
              for q in range(4)]
    for cp in lloads:
        cp.start()
    tcols = pl.ds(pl.multiple_of(2048 * y, 2048), 2048)
    tloads = [pltpu.make_async_copy(t_hbm.at[pl.ds(32 * q, 32), tcols], Tq.at[q, y], ld.at[8 + q])
              for q in range(4)]
    for cp in tloads:
        cp.start()

    bar = pltpu.get_barrier_semaphore()
    D_y2, D_x2 = dev(y_=y2), dev(x_=x2)
    peers = [D_yp, D_ym, D_xp, D_xm, D_sib, D_zh, D_y2, D_x2,
             dev(z_=(zl + 1) % 4), dev(z_=(zl + 3) % 4)]
    for p in peers:
        pl.semaphore_signal(bar, inc=1, device_id=p, device_id_type=MESH)
    pl.semaphore_wait(bar, len(peers))

    pending = []

    def send(src, sems, n, rs, d, cond=None):
        cp = pltpu.make_async_remote_copy(
            src_ref=src, dst_ref=src, send_sem=sems.at[n], recv_sem=rs,
            device_id=d, device_id_type=MESH)
        if cond is None:
            cp.start()
        else:
            pl.when(cond)(cp.start)
        pending.append((src, sems.at[n], cond))

    def wait_recv(ref, rs):
        pltpu.make_async_remote_copy(
            src_ref=ref, dst_ref=ref, send_sem=rs, recv_sem=rs,
            device_id=D_sib, device_id_type=MESH).wait_recv()

    zorder = [zl, 1 + zl % 2, (2 + 3 * zl) % 5, 3 - 3 * (zl // 2)]

    zinfo = []
    for zb in zorder:
        right = zb < zl
        zinfo.append((zb, jnp.where(right, zl < 3, zl > 0),
                      dev(z_=jnp.clip(zl + jnp.where(right, 1, -1), 0, 3))))

    mid = (zl + 1) // 2 == 1

    class Rho:
        def __init__(self, buf, rows, ss, rs):
            self.buf, self.half, self.ss, self.rs = buf, rows // 2, ss, rs
            self.keys, self.done = {}, set()

        def at(self, i, h):
            return self.buf.at[i, pl.ds(h * self.half, self.half)]

        def send(self, key, src, rs, d, cond=None):
            k = self.keys.setdefault(key, len(self.keys))
            cp = pltpu.make_async_remote_copy(
                src_ref=src, dst_ref=src, send_sem=self.ss.at[k], recv_sem=rs,
                device_id=d, device_id_type=MESH)
            if cond is None:
                cp.start()
            else:
                pl.when(cond)(cp.start)
            if key not in self.done:
                self.done.add(key)
                pending.append(((self.buf, None if key[1] == "s" else self.half), (self.ss, k), cond))

        def put(self, key, i, h, d, cond=None):
            self.send((key, h), self.at(i, h), self.rs.at[h, i], d, cond)

        def sib(self, key, i):
            self.send((key, "s"), self.buf.at[i], self.rs.at[0, i], D_sib)

        def got(self, i, h):
            wait_recv(self.at(i, h), self.rs.at[h, i])

        def own(self, hs=None):
            for h in (range(2) if hs is None else (hs,)):
                self.put("or", me, h, D_zr, zl < 3)
                self.put("ol", me, h, D_zl, zl > 0)
                self.put("oa", me, h, D_yp if h == 0 else D_ym)
                self.put("ob", me, h, D_ym if h == 0 else D_yp)
            if hs != 0:
                self.sib("o", me)

        def zpart(self, j, h):
            zb, ok, d = zinfo[j]
            i = rid(y, zb, c)
            self.got(i, h)
            self.put(("z", j), i, h, d, ok)
            self.put(("za", j), i, h, D_yp if h == 0 else D_ym)
            self.put(("zb", j), i, h, D_ym if h == 0 else D_yp)

        def zsib(self, j):
            self.sib(("z", j), rid(y, zorder[j], c))

        def Z(self, j):
            self.zpart(j, 0)
            self.zpart(j, 1)
            self.zsib(j)

        def Z12(self):
            self.zpart(1, 0)
            self.zpart(2, 0)
            self.zpart(1, 1)
            self.zpart(2, 1)
            self.zsib(1)
            self.zsib(2)

        def Y(self, j):
            a, b = rid(ym, zorder[j], c), rid(yp, zorder[j], c)
            self.got(a, 0)
            self.put(("ya", j), a, 0, D_yp)
            self.got(b, 1)
            self.put(("yb", j), b, 1, D_ym)
            self.got(a, 1)
            self.sib(("ya", j), a)
            self.got(b, 0)
            self.sib(("yb", j), b)

        def Y2(self, j):
            i = rid(y2, zorder[j], c)
            self.got(i, 0)
            self.got(i, 1)
            self.sib(("y2", j), i)

        def zy(self):
            @pl.when(mid)
            def _():
                self.Z12()
                self.Y(0)
                self.Z(3)

            @pl.when(jnp.logical_not(mid))
            def _():
                self.Z(1)
                self.Y(0)
                self.Z(2)
                self.Y(1)
                self.Z(3)

        def zya(self):
            @pl.when(mid)
            def _():
                self.Z12()

            @pl.when(jnp.logical_not(mid))
            def _():
                self.Z(1)
                self.Y(0)

        def zyb(self):
            @pl.when(mid)
            def _():
                self.Y(0)
                self.Z(3)

            @pl.when(jnp.logical_not(mid))
            def _():
                self.Z(2)
                self.Y(1)
                self.Z(3)

        def y1(self):
            @pl.when((zl + 1) // 2 == 1)
            def _():
                self.Y(1)


        def S(self, yy):
            for j in range(4):
                i = rid(yy, zorder[j], 1 - c)
                wait_recv(self.buf.at[i], self.rs.at[0, i])

    class Gamma:
        def __init__(self, buf, ss, rs, parts):
            self.buf, self.ss, self.rs, self.parts, self.n = buf, ss, rs, parts, 0

        def put(self, i, p, d):
            send(self.buf.at[i, p], self.ss, self.n, self.rs.at[p, i], d)
            self.n += 1

        def got(self, i, p):
            wait_recv(self.buf.at[i, p], self.rs.at[p, i])

        def own_zh(self, p):
            self.put(col, p, D_zh)

        def own_x(self, p):
            self.put(col, p, D_xp if p % 2 == 0 else D_xm)
            self.put(col, p, D_xm if p % 2 == 0 else D_xp)

        def partner(self, p):
            i = x * 2 + 1 - zh
            self.got(i, p)
            self.put(i, p, D_xp if p % 2 == 0 else D_xm)
            self.put(i, p, D_xm if p % 2 == 0 else D_xp)

        def ring(self, b, p):
            hb = zh if b == 0 else 1 - zh
            if p % 2 == 0:
                self.got(xm * 2 + hb, p)
                self.put(xm * 2 + hb, p, D_xp)
            else:
                self.got(xp * 2 + hb, p)
                self.put(xp * 2 + hb, p, D_xm)

        def rest(self, b, p):
            hb = zh if b == 0 else 1 - zh
            self.got((xp if p % 2 == 0 else xm) * 2 + hb, p)
            self.got(x2 * 2 + hb, p)


    class Tok:
        n = 0

        def own_y(self, r):
            if True:
                for q, d in ((yp, D_yp), (ym, D_ym), (y2, D_y2)):
                    cp = pltpu.make_async_remote_copy(
                        src_ref=t_hbm.at[pl.ds(pl.multiple_of(32 * r, 32), 32),
                                         pl.ds(pl.multiple_of(2048 * q, 2048), 2048)],
                        dst_ref=Tq.at[r, y], send_sem=st.at[self.n], recv_sem=rt.at[r, y],
                        device_id=d, device_id_type=MESH)
                    cp.start()
                    self.n += 1
                    pending.append((cp.src_ref, cp.src_sem, None))

        def share_x(self, q):
            wait_recv(Tq.at[x, q], rt.at[x, q])
            for d in (D_xp, D_xm):
                send(Tq.at[x, q], st, self.n, rt.at[x, q], d)
                self.n += 1

        def rest(self):
            for r in (xp, xm, x2):
                for q in (yp, ym, y2):
                    wait_recv(Tq.at[r, q], rt.at[r, q])

    class Nar:
        keys = {}

        def send(self, key, src, rs, d, cond=None):
            fresh = key not in self.keys
            k = self.keys.setdefault(key, len(self.keys))
            cp = pltpu.make_async_remote_copy(
                src_ref=src, dst_ref=src, send_sem=sn.at[k], recv_sem=rs,
                device_id=d, device_id_type=MESH)
            if cond is None:
                cp.start()
            else:
                pl.when(cond)(cp.start)
            if fresh:
                pending.append(((Np, None if key[1] == "s" else 128), (sn, k), cond))

        def put(self, key, i, h, d, cond):
            self.send((key, h), Np.at[i, pl.ds(128 * h, 128)], rn.at[h, i], d, cond)

        def sib(self, j):
            i = 2 * zorder[j] + c
            self.send((j, "s"), Np.at[i], rn.at[0, i], D_sib)

        def own(self, h):
            i = 2 * zl + c
            self.put("r", i, h, D_zr, zl < 3)
            self.put("l", i, h, D_zl, zl > 0)
            if h == 1:
                self.sib(0)

        def zpart(self, j, h):
            zb, ok, d = zinfo[j]
            i = 2 * zb + c
            wait_recv(Np.at[i, pl.ds(128 * h, 128)], rn.at[h, i])
            self.put(("z", j), i, h, d, ok)
            if h == 1:
                self.sib(j)

        def S(self, j):
            i = 2 * zorder[j] + 1 - c
            wait_recv(Np.at[i], rn.at[0, i])

        def dots(self, js):
            for j in js:
                self.S(j)
                out_dot(j, j == 0)

        def all(self):
            for j in (1, 2, 3):
                self.zpart(j, 0)
            self.zpart(1, 1)
            self.zpart(2, 1)

            @pl.when(mid)
            def _():
                self.zpart(3, 1)
                T.rest()
                self.dots((0, 1, 2, 3))

            @pl.when(jnp.logical_not(mid))
            def _():
                T.rest()
                self.dots((0, 1, 2))
                self.zpart(3, 1)
                self.dots((3,))

    R = Rho(Rp, 128, sr, rr)
    X = Rho(Xp, 256, sx, rx)
    N = Nar()
    T = Tok()
    G = Gamma(Gp, sg, rg, 2)
    L = Gamma(Lp, sl, rl, 4)


    def x_part(h, hb):
        @pl.loop(0, 4)
        def _(q):
            k = 2 * q + hb
            acc[pl.ds(128 * h, 128)] += jnp.dot(
                Gp[k, h], Rp[pl.ds(4 * k, 4)].reshape(512, 512), preferred_element_type=F32)

    def x_done(h):
        Xp[me, pl.ds(128 * h, 128)] = acc[pl.ds(128 * h, 128)].astype(BF)
        acc[pl.ds(128 * h, 128)] = jnp.zeros((128, 512), F32)
        X.own(h)

    def p(h, yy):
        @pl.loop(0, 2)
        def _(i):
            k = 2 * yy + i
            acc[pl.ds(128 * h, 128)] += jnp.dot(
                Lp[k, pl.ds(2 * h, 2)].reshape(128, 1024),
                Xp[pl.ds(4 * k, 4)].reshape(1024, 512), preferred_element_type=F32)

    stores = []

    def finish_rows(h):
        rows = pl.ds(128 * h, 128)
        nw = Wv[rows] - 0.01 * acc[rows]
        Np[2 * zl + c, rows] = nw.astype(BF)
        N.own(h)
        Wv[rows] = nw
        cp = pltpu.make_async_copy(Wv.at[rows], nw_hbm.at[rows], ld.at[6 + h])
        cp.start()
        stores.append(cp)

    def out_dot(j, first):
        zb = zorder[j]
        lhs = Tq[:, :, :, pl.ds(pl.multiple_of(512 * zb, 512), 512)].reshape(512, 512)
        v = jnp.dot(lhs, Np[pl.ds(2 * zb, 2)].reshape(512, 512), preferred_element_type=F32)
        if first:
            oacc[...] = v
        else:
            oacc[...] += v

    acc[...] = jnp.zeros_like(acc)
    loads[0].wait()
    loads[1].wait()
    loads[3].wait()
    G.own_zh(0)
    R.own()
    G.own_x(0)
    G.own_x(1)
    T.own_y(x)
    G.partner(0)
    R.zy()
    for cp in lloads: cp.wait()
    G.own_zh(1)
    G.ring(0, 0)
    G.ring(0, 1)
    R.y1()
    R.Y2(0)
    G.ring(1, 0)
    L.own_x(0)
    L.own_x(1)
    R.Y(2)
    R.Y2(1)
    R.Y(3)
    R.Y2(2)
    G.partner(1)
    L.own_zh(0)
    L.own_zh(1)
    R.Y2(3)
    R.S(y)
    R.S(ym)
    R.S(yp)
    R.S(y2)
    G.rest(0, 0)
    G.rest(1, 0)
    x_part(0, zh)
    x_part(0, 1 - zh)
    x_done(0)
    G.ring(1, 1)
    G.rest(0, 1)
    x_part(1, zh)
    G.rest(1, 1)
    x_part(1, 1 - zh)
    x_done(1)
    L.own_x(2)
    L.own_x(3)
    L.ring(0, 0)
    L.ring(0, 1)
    L.partner(0)
    X.zya()
    L.partner(1)
    X.zyb()
    L.own_zh(2)
    L.ring(0, 2)
    L.ring(0, 3)
    X.y1()
    X.Y2(0)
    L.own_zh(3)
    X.Y(2)
    L.ring(1, 0)
    L.ring(1, 1)
    L.partner(2)
    X.Y2(1)
    X.Y(3)
    L.ring(1, 2)
    L.rest(0, 0)
    L.rest(0, 1)
    L.rest(1, 0)
    L.rest(1, 1)
    L.partner(3)
    X.S(y)
    p(0, y)
    X.S(ym)
    p(0, ym)
    X.Y2(2)
    X.S(yp)
    p(0, yp)
    X.Y2(3)
    T.own_y(x2)
    L.ring(1, 3)
    X.S(y2)
    p(0, y2)
    loads[2].wait()
    finish_rows(0)
    L.rest(0, 2)
    L.rest(0, 3)
    L.rest(1, 2)
    p(1, x)
    p(1, xp)
    L.rest(1, 3)
    T.share_x(yp)
    T.share_x(ym)
    T.share_x(y2)
    p(1, xm)
    p(1, x2)
    finish_rows(1)
    for cp in tloads: cp.wait()
    N.all()
    part = oacc[...].reshape(4, 4, 32, 512)
    for q in range(4):
        Ob[q] = part[:, q].reshape(128, 512).astype(BF)
    for k, (q, d) in enumerate(((y2, D_y2), (yp, D_yp), (ym, D_ym))):
        cp = pltpu.make_async_remote_copy(
            src_ref=Ob.at[q], dst_ref=Ib.at[y], send_sem=so.at[k], recv_sem=ro.at[y],
            device_id=d, device_id_type=MESH)
        cp.start()
        pending.append((cp.src_ref, cp.src_sem, None))
    for q in range(4):
        @pl.when(q == y)
        def _(q=q):
            acc[pl.ds(0, 128)] = oacc[...].reshape(4, 4, 32, 512)[:, q].reshape(128, 512)
    for q in (yp, ym, y2):
      wait_recv(Ib.at[q], ro.at[q])
    Ov[...] = (acc[pl.ds(0, 128)] + Ib[yp].astype(F32) + Ib[ym].astype(F32)
              + Ib[y2].astype(F32)).astype(BF)
    store_out = pltpu.make_async_copy(Ov, out_hbm, ld.at[3])
    store_out.start()
    for src, sem, cond in pending:
        if isinstance(src, tuple):
            src = src[0].at[0] if src[1] is None else src[0].at[0, pl.ds(0, src[1])]
            sem = sem[0].at[sem[1]]
        cp = pltpu.make_async_remote_copy(
            src_ref=src, dst_ref=src, send_sem=sem, recv_sem=sem,
            device_id=D_sib, device_id_type=MESH)
        if cond is None:
            cp.wait_send()
        else:
            pl.when(cond)(cp.wait_send)
    for cp in stores:
        cp.wait()
    store_out.wait()


def place(a_hbm, b_hbm, c_hbm, d_hbm, a, b, sem):
    parts = [(a_hbm, a, c_hbm, pl.ds(64 * q, 64)) for q in range(4)] + [(b_hbm, b, d_hbm, pl.ds(0, 128))]
    takes = [pltpu.make_async_copy(s.at[r], v.at[r], sem.at[k]) for k, (s, v, o, r) in enumerate(parts)]
    puts = [pltpu.make_async_copy(v.at[r], o.at[r], sem.at[5 + k]) for k, (s, v, o, r) in enumerate(parts)]
    for cp in takes:
        cp.start()
    for t, p in zip(takes, puts):
        t.wait()
        p.start()
    for cp in puts:
        cp.wait()


def shards(weight, grad, left, right, tokens):
    any_ = pl.BlockSpec(memory_space=pl.ANY)
    dma = pltpu.SemaphoreType.DMA
    new_weight, output = pl.pallas_call(
        kernel,
        out_shape=(jax.ShapeDtypeStruct((256, 512), F32), jax.ShapeDtypeStruct((128, 512), BF)),
        in_specs=[any_] * 5,
        out_specs=(any_, any_),
        scratch_shapes=[
            pltpu.VMEM((8, 2, 128, 512), BF),
            pltpu.VMEM((32, 128, 512), BF),
            pltpu.VMEM((8, 4, 64, 1024), BF),
            pltpu.VMEM((32, 256, 512), BF),
            pltpu.VMEM((8, 256, 512), BF),
            pltpu.VMEM((4, 4, 32, 2048), BF),
            pltpu.VMEM((256, 512), F32),
            pltpu.VMEM((128, 512), BF),
            pltpu.VMEM((256, 512), F32),
            pltpu.VMEM((512, 512), F32),
            pltpu.VMEM((4, 128, 512), BF),
            pltpu.VMEM((4, 128, 512), BF),
            dma((16,)), dma((52,)), dma((16,)), dma((28,)), dma((52,)), dma((20,)), dma((12,)), dma((4,)),
            dma((2, 32)), dma((2, 8)), dma((4, 8)), dma((2, 32)), dma((2, 8)), dma((4, 4)), dma((4,)),
        ],
        compiler_params=pltpu.CompilerParams(
            collective_id=0, has_side_effects=True, vmem_limit_bytes=56 * 2**20),
    )(weight, grad, left, right, tokens)
    return pl.pallas_call(
        place,
        out_shape=(jax.ShapeDtypeStruct((256, 512), F32), jax.ShapeDtypeStruct((128, 512), BF)),
        in_specs=[any_] * 2,
        out_specs=(any_, any_),
        scratch_shapes=[pltpu.VMEM((256, 512), F32), pltpu.VMEM((128, 512), BF), dma((10,))],
    )(new_weight, output)


def solution(mesh):
    return jax.shard_map(
        shards,
        mesh=mesh,
        in_specs=(
            P("row", "col"),
            P("row", "col"),
            P("row", "col"),
            P("row", "col"),
            P("row", None),
        ),
        out_specs=(P("row", "col"), P("row", "col")),
        check_vma=False,
    )
```

```python
import jax
import jax.numpy as jnp
from jax import lax
from jax.experimental import pallas as pl
from jax.experimental.pallas import tpu as pltpu
from jax.sharding import PartitionSpec as P

MESH = pl.DeviceIdType.MESH
BF = jnp.bfloat16
F32 = jnp.float32


def kernel(w_hbm, g_hbm, l_hbm, r_hbm, t_hbm, nw_hbm, out_hbm,
           Gp, Rp, Lp, Xp, Np, Tq, Wv, Ov, acc, oacc, Ob, Ib,
           ld, sr, sg, sl, sx, sn, st, so, rr, rg, rl, rx, rn, rt, ro):
    row, col = lax.axis_index("row"), lax.axis_index("col")
    y, zl, c = row // 8, (row // 2) % 4, row % 2
    x, zh = col // 2, col % 2
    yp, ym, y2 = (y + 1) % 4, (y + 3) % 4, (y + 2) % 4
    xp, xm, x2 = (x + 1) % 4, (x + 3) % 4, (x + 2) % 4

    def rid(y_, z_, c_):
        return (y_ * 4 + z_) * 2 + c_

    def dev(y_=y, z_=zl, c_=c, x_=x, h_=zh):
        return (rid(y_, z_, c_), x_ * 2 + h_)

    D_yp, D_ym = dev(y_=yp), dev(y_=ym)
    D_xp, D_xm = dev(x_=xp), dev(x_=xm)
    D_sib, D_zh = dev(c_=1 - c), dev(h_=1 - zh)
    D_zr, D_zl = dev(z_=jnp.minimum(zl + 1, 3)), dev(z_=jnp.maximum(zl - 1, 0))
    me = row

    loads = [
        pltpu.make_async_copy(r_hbm, Rp.at[me], ld.at[0]),
        pltpu.make_async_copy(g_hbm.at[pl.ds(0, 128)], Gp.at[col, 0], ld.at[1]),
        pltpu.make_async_copy(w_hbm, Wv, ld.at[5]),
        pltpu.make_async_copy(g_hbm.at[pl.ds(128, 128)], Gp.at[col, 1], ld.at[4]),
    ]
    for cp in loads:
        cp.start()
    lloads = [pltpu.make_async_copy(l_hbm.at[pl.ds(64 * q, 64)], Lp.at[col, q], ld.at[12 + q])
              for q in range(4)]
    for cp in lloads:
        cp.start()
    tcols = pl.ds(pl.multiple_of(2048 * y, 2048), 2048)
    tloads = [pltpu.make_async_copy(t_hbm.at[pl.ds(32 * q, 32), tcols], Tq.at[q, y], ld.at[8 + q])
              for q in range(4)]
    for cp in tloads:
        cp.start()

    bar = pltpu.get_barrier_semaphore()
    D_y2, D_x2 = dev(y_=y2), dev(x_=x2)
    peers = [D_yp, D_ym, D_xp, D_xm, D_sib, D_zh, D_y2, D_x2,
             dev(z_=(zl + 1) % 4), dev(z_=(zl + 3) % 4)]
    for p in peers:
        pl.semaphore_signal(bar, inc=1, device_id=p, device_id_type=MESH)
    pl.semaphore_wait(bar, len(peers))

    pending = []

    def send(src, sems, n, rs, d, cond=None):
        cp = pltpu.make_async_remote_copy(
            src_ref=src, dst_ref=src, send_sem=sems.at[n], recv_sem=rs,
            device_id=d, device_id_type=MESH)
        if cond is None:
            cp.start()
        else:
            pl.when(cond)(cp.start)
        pending.append((src, sems.at[n], cond))

    def wait_recv(ref, rs):
        pltpu.make_async_remote_copy(
            src_ref=ref, dst_ref=ref, send_sem=rs, recv_sem=rs,
            device_id=D_sib, device_id_type=MESH).wait_recv()

    zorder = [zl, 1 + zl % 2, (2 + 3 * zl) % 5, 3 - 3 * (zl // 2)]

    zinfo = []
    for zb in zorder:
        right = zb < zl
        zinfo.append((zb, jnp.where(right, zl < 3, zl > 0),
                      dev(z_=jnp.clip(zl + jnp.where(right, 1, -1), 0, 3))))

    mid = (zl + 1) // 2 == 1

    class Rho:
        def __init__(self, buf, rows, ss, rs):
            self.buf, self.half, self.ss, self.rs = buf, rows // 2, ss, rs
            self.keys, self.done = {}, set()

        def at(self, i, h):
            return self.buf.at[i, pl.ds(h * self.half, self.half)]

        def send(self, key, src, rs, d, cond=None):
            k = self.keys.setdefault(key, len(self.keys))
            cp = pltpu.make_async_remote_copy(
                src_ref=src, dst_ref=src, send_sem=self.ss.at[k], recv_sem=rs,
                device_id=d, device_id_type=MESH)
            if cond is None:
                cp.start()
            else:
                pl.when(cond)(cp.start)
            if key not in self.done:
                self.done.add(key)
                pending.append(((self.buf, None if key[1] == "s" else self.half), (self.ss, k), cond))

        def put(self, key, i, h, d, cond=None):
            self.send((key, h), self.at(i, h), self.rs.at[h, i], d, cond)

        def sib(self, key, i):
            self.send((key, "s"), self.buf.at[i], self.rs.at[0, i], D_sib)

        def got(self, i, h):
            wait_recv(self.at(i, h), self.rs.at[h, i])

        def own(self, hs=None):
            for h in (range(2) if hs is None else (hs,)):
                self.put("or", me, h, D_zr, zl < 3)
                self.put("ol", me, h, D_zl, zl > 0)
                self.put("oa", me, h, D_yp if h == 0 else D_ym)
                self.put("ob", me, h, D_ym if h == 0 else D_yp)
            if hs != 0:
                self.sib("o", me)

        def zpart(self, j, h):
            zb, ok, d = zinfo[j]
            i = rid(y, zb, c)
            self.got(i, h)
            self.put(("z", j), i, h, d, ok)
            self.put(("za", j), i, h, D_yp if h == 0 else D_ym)
            self.put(("zb", j), i, h, D_ym if h == 0 else D_yp)

        def zsib(self, j):
            self.sib(("z", j), rid(y, zorder[j], c))

        def Z(self, j):
            self.zpart(j, 0)
            self.zpart(j, 1)
            self.zsib(j)

        def Z12(self):
            self.zpart(1, 0)
            self.zpart(2, 0)
            self.zpart(1, 1)
            self.zpart(2, 1)
            self.zsib(1)
            self.zsib(2)

        def Y(self, j):
            a, b = rid(ym, zorder[j], c), rid(yp, zorder[j], c)
            self.got(a, 0)
            self.put(("ya", j), a, 0, D_yp)
            self.got(b, 1)
            self.put(("yb", j), b, 1, D_ym)
            self.got(a, 1)
            self.sib(("ya", j), a)
            self.got(b, 0)
            self.sib(("yb", j), b)

        def Y2(self, j):
            i = rid(y2, zorder[j], c)
            self.got(i, 0)
            self.got(i, 1)
            self.sib(("y2", j), i)

        def zy(self):
            @pl.when(mid)
            def _():
                self.Z12()
                self.Y(0)
                self.Z(3)

            @pl.when(jnp.logical_not(mid))
            def _():
                self.Z(1)
                self.Y(0)
                self.Z(2)
                self.Y(1)
                self.Z(3)

        def zya(self):
            @pl.when(mid)
            def _():
                self.Z12()

            @pl.when(jnp.logical_not(mid))
            def _():
                self.Z(1)
                self.Y(0)

        def zyb(self):
            @pl.when(mid)
            def _():
                self.Y(0)
                self.Z(3)

            @pl.when(jnp.logical_not(mid))
            def _():
                self.Z(2)
                self.Y(1)
                self.Z(3)

        def y1(self):
            @pl.when((zl + 1) // 2 == 1)
            def _():
                self.Y(1)


        def S(self, yy):
            for j in range(4):
                i = rid(yy, zorder[j], 1 - c)
                wait_recv(self.buf.at[i], self.rs.at[0, i])

    class Gamma:
        def __init__(self, buf, ss, rs, parts):
            self.buf, self.ss, self.rs, self.parts, self.n = buf, ss, rs, parts, 0

        def put(self, i, p, d):
            send(self.buf.at[i, p], self.ss, self.n, self.rs.at[p, i], d)
            self.n += 1

        def got(self, i, p):
            wait_recv(self.buf.at[i, p], self.rs.at[p, i])

        def own_zh(self, p):
            self.put(col, p, D_zh)

        def own_x(self, p):
            self.put(col, p, D_xp if p % 2 == 0 else D_xm)
            self.put(col, p, D_xm if p % 2 == 0 else D_xp)

        def partner(self, p):
            i = x * 2 + 1 - zh
            self.got(i, p)
            self.put(i, p, D_xp if p % 2 == 0 else D_xm)
            self.put(i, p, D_xm if p % 2 == 0 else D_xp)

        def ring(self, b, p):
            hb = zh if b == 0 else 1 - zh
            if p % 2 == 0:
                self.got(xm * 2 + hb, p)
                self.put(xm * 2 + hb, p, D_xp)
            else:
                self.got(xp * 2 + hb, p)
                self.put(xp * 2 + hb, p, D_xm)

        def rest(self, b, p):
            hb = zh if b == 0 else 1 - zh
            self.got((xp if p % 2 == 0 else xm) * 2 + hb, p)
            self.got(x2 * 2 + hb, p)


    class Tok:
        n = 0

        def own_y(self, r):
            if True:
                for q, d in ((yp, D_yp), (ym, D_ym), (y2, D_y2)):
                    cp = pltpu.make_async_remote_copy(
                        src_ref=t_hbm.at[pl.ds(pl.multiple_of(32 * r, 32), 32),
                                         pl.ds(pl.multiple_of(2048 * q, 2048), 2048)],
                        dst_ref=Tq.at[r, y], send_sem=st.at[self.n], recv_sem=rt.at[r, y],
                        device_id=d, device_id_type=MESH)
                    cp.start()
                    self.n += 1
                    pending.append((cp.src_ref, cp.src_sem, None))

        def share_x(self, q):
            wait_recv(Tq.at[x, q], rt.at[x, q])
            for d in (D_xp, D_xm):
                send(Tq.at[x, q], st, self.n, rt.at[x, q], d)
                self.n += 1

        def rest(self):
            for r in (xp, xm, x2):
                for q in (yp, ym, y2):
                    wait_recv(Tq.at[r, q], rt.at[r, q])

    class Nar:
        keys = {}

        def send(self, key, src, rs, d, cond=None):
            fresh = key not in self.keys
            k = self.keys.setdefault(key, len(self.keys))
            cp = pltpu.make_async_remote_copy(
                src_ref=src, dst_ref=src, send_sem=sn.at[k], recv_sem=rs,
                device_id=d, device_id_type=MESH)
            if cond is None:
                cp.start()
            else:
                pl.when(cond)(cp.start)
            if fresh:
                pending.append(((Np, None if key[1] == "s" else 128), (sn, k), cond))

        def put(self, key, i, h, d, cond):
            self.send((key, h), Np.at[i, pl.ds(128 * h, 128)], rn.at[h, i], d, cond)

        def sib(self, j):
            i = 2 * zorder[j] + c
            self.send((j, "s"), Np.at[i], rn.at[0, i], D_sib)

        def own(self, h):
            i = 2 * zl + c
            self.put("r", i, h, D_zr, zl < 3)
            self.put("l", i, h, D_zl, zl > 0)
            if h == 1:
                self.sib(0)

        def zpart(self, j, h):
            zb, ok, d = zinfo[j]
            i = 2 * zb + c
            wait_recv(Np.at[i, pl.ds(128 * h, 128)], rn.at[h, i])
            self.put(("z", j), i, h, d, ok)
            if h == 1:
                self.sib(j)

        def S(self, j):
            i = 2 * zorder[j] + 1 - c
            wait_recv(Np.at[i], rn.at[0, i])

        def dots(self, js):
            for j in js:
                self.S(j)
                out_dot(j, j == 0)

        def all(self):
            for j in (1, 2, 3):
                self.zpart(j, 0)
            self.zpart(1, 1)
            self.zpart(2, 1)

            @pl.when(mid)
            def _():
                self.zpart(3, 1)
                T.rest()
                self.dots((0, 1, 2, 3))

            @pl.when(jnp.logical_not(mid))
            def _():
                T.rest()
                self.dots((0, 1, 2))
                self.zpart(3, 1)
                self.dots((3,))

    R = Rho(Rp, 128, sr, rr)
    X = Rho(Xp, 256, sx, rx)
    N = Nar()
    T = Tok()
    G = Gamma(Gp, sg, rg, 2)
    L = Gamma(Lp, sl, rl, 4)


    def x_part(h, hb):
        lhs = jnp.concatenate([Gp[2 * q + hb, h] for q in range(4)], axis=1)
        rhs = jnp.concatenate(
            [Rp[pl.ds(4 * (2 * q + hb), 4)].reshape(512, 512) for q in range(4)], axis=0)
        acc[pl.ds(128 * h, 128)] += jnp.dot(lhs, rhs, preferred_element_type=F32)

    def x_done(h):
        Xp[me, pl.ds(128 * h, 128)] = acc[pl.ds(128 * h, 128)].astype(BF)
        acc[pl.ds(128 * h, 128)] = jnp.zeros((128, 512), F32)
        X.own(h)

    def p(h, yy):
        rows = pl.ds(2 * h, 2)
        lhs = jnp.concatenate(
            [Lp[2 * yy + i, rows].reshape(128, 1024) for i in range(2)], axis=1)
        acc[pl.ds(128 * h, 128)] += jnp.dot(
            lhs, Xp[pl.ds(8 * yy, 8)].reshape(2048, 512), preferred_element_type=F32)

    stores = []

    def finish_rows(h):
        rows = pl.ds(128 * h, 128)
        nw = Wv[rows] - 0.01 * acc[rows]
        Np[2 * zl + c, rows] = nw.astype(BF)
        N.own(h)
        Wv[rows] = nw
        cp = pltpu.make_async_copy(Wv.at[rows], nw_hbm.at[rows], ld.at[6 + h])
        cp.start()
        stores.append(cp)

    def out_dot(j, first):
        zb = zorder[j]
        lhs = Tq[:, :, :, pl.ds(pl.multiple_of(512 * zb, 512), 512)].reshape(512, 512)
        v = jnp.dot(lhs, Np[pl.ds(2 * zb, 2)].reshape(512, 512), preferred_element_type=F32)
        if first:
            oacc[...] = v
        else:
            oacc[...] += v

    acc[...] = jnp.zeros_like(acc)
    loads[0].wait()
    loads[1].wait()
    loads[3].wait()
    G.own_zh(0)
    R.own()
    G.own_x(0)
    G.own_x(1)
    T.own_y(x)
    G.partner(0)
    R.zy()
    for cp in lloads: cp.wait()
    G.own_zh(1)
    G.ring(0, 0)
    G.ring(0, 1)
    R.y1()
    R.Y2(0)
    G.ring(1, 0)
    L.own_x(0)
    L.own_x(1)
    R.Y(2)
    R.Y2(1)
    R.Y(3)
    R.Y2(2)
    G.partner(1)
    L.own_zh(0)
    L.own_zh(1)
    R.Y2(3)
    R.S(y)
    R.S(ym)
    R.S(yp)
    R.S(y2)
    G.rest(0, 0)
    G.rest(1, 0)
    x_part(0, zh)
    x_part(0, 1 - zh)
    x_done(0)
    G.ring(1, 1)
    G.rest(0, 1)
    x_part(1, zh)
    G.rest(1, 1)
    x_part(1, 1 - zh)
    x_done(1)
    L.own_x(2)
    L.own_x(3)
    L.ring(0, 0)
    L.ring(0, 1)
    L.partner(0)
    X.zya()
    L.partner(1)
    X.zyb()
    L.own_zh(2)
    L.ring(0, 2)
    L.ring(0, 3)
    X.y1()
    X.Y2(0)
    L.own_zh(3)
    X.Y(2)
    L.ring(1, 0)
    L.ring(1, 1)
    L.partner(2)
    X.Y2(1)
    X.Y(3)
    L.ring(1, 2)
    L.rest(0, 0)
    L.rest(0, 1)
    L.rest(1, 0)
    L.rest(1, 1)
    L.partner(3)
    X.S(y)
    p(0, y)
    X.S(ym)
    p(0, ym)
    X.Y2(2)
    X.S(yp)
    p(0, yp)
    X.Y2(3)
    T.own_y(x2)
    L.ring(1, 3)
    X.S(y2)
    p(0, y2)
    loads[2].wait()
    finish_rows(0)
    L.rest(0, 2)
    L.rest(0, 3)
    L.rest(1, 2)
    p(1, x)
    p(1, xp)
    L.rest(1, 3)
    p(1, xm)
    p(1, x2)
    finish_rows(1)
    T.share_x(yp)
    T.share_x(ym)
    T.share_x(y2)
    for cp in tloads: cp.wait()
    N.all()
    part = oacc[...].reshape(4, 4, 32, 512)
    for q in range(4):
        Ob[q] = part[:, q].reshape(128, 512).astype(BF)
    for k, (q, d) in enumerate(((y2, D_y2), (yp, D_yp), (ym, D_ym))):
        cp = pltpu.make_async_remote_copy(
            src_ref=Ob.at[q], dst_ref=Ib.at[y], send_sem=so.at[k], recv_sem=ro.at[y],
            device_id=d, device_id_type=MESH)
        cp.start()
        pending.append((cp.src_ref, cp.src_sem, None))
    for q in range(4):
        @pl.when(q == y)
        def _(q=q):
            acc[pl.ds(0, 128)] = oacc[...].reshape(4, 4, 32, 512)[:, q].reshape(128, 512)
    for q in (yp, ym, y2):
      wait_recv(Ib.at[q], ro.at[q])
    Ov[...] = (acc[pl.ds(0, 128)] + Ib[yp].astype(F32) + Ib[ym].astype(F32)
              + Ib[y2].astype(F32)).astype(BF)
    store_out = pltpu.make_async_copy(Ov, out_hbm, ld.at[3])
    store_out.start()
    for src, sem, cond in pending:
        if isinstance(src, tuple):
            src = src[0].at[0] if src[1] is None else src[0].at[0, pl.ds(0, src[1])]
            sem = sem[0].at[sem[1]]
        cp = pltpu.make_async_remote_copy(
            src_ref=src, dst_ref=src, send_sem=sem, recv_sem=sem,
            device_id=D_sib, device_id_type=MESH)
        if cond is None:
            cp.wait_send()
        else:
            pl.when(cond)(cp.wait_send)
    for cp in stores:
        cp.wait()
    store_out.wait()


def place(a_hbm, b_hbm, c_hbm, d_hbm, a, b, sem):
    parts = [(a_hbm, a, c_hbm, pl.ds(64 * q, 64)) for q in range(4)] + [(b_hbm, b, d_hbm, pl.ds(0, 128))]
    takes = [pltpu.make_async_copy(s.at[r], v.at[r], sem.at[k]) for k, (s, v, o, r) in enumerate(parts)]
    puts = [pltpu.make_async_copy(v.at[r], o.at[r], sem.at[5 + k]) for k, (s, v, o, r) in enumerate(parts)]
    for cp in takes:
        cp.start()
    for t, p in zip(takes, puts):
        t.wait()
        p.start()
    for cp in puts:
        cp.wait()


def shards(weight, grad, left, right, tokens):
    any_ = pl.BlockSpec(memory_space=pl.ANY)
    dma = pltpu.SemaphoreType.DMA
    new_weight, output = pl.pallas_call(
        kernel,
        out_shape=(jax.ShapeDtypeStruct((256, 512), F32), jax.ShapeDtypeStruct((128, 512), BF)),
        in_specs=[any_] * 5,
        out_specs=(any_, any_),
        scratch_shapes=[
            pltpu.VMEM((8, 2, 128, 512), BF),
            pltpu.VMEM((32, 128, 512), BF),
            pltpu.VMEM((8, 4, 64, 1024), BF),
            pltpu.VMEM((32, 256, 512), BF),
            pltpu.VMEM((8, 256, 512), BF),
            pltpu.VMEM((4, 4, 32, 2048), BF),
            pltpu.VMEM((256, 512), F32),
            pltpu.VMEM((128, 512), BF),
            pltpu.VMEM((256, 512), F32),
            pltpu.VMEM((512, 512), F32),
            pltpu.VMEM((4, 128, 512), BF),
            pltpu.VMEM((4, 128, 512), BF),
            dma((16,)), dma((52,)), dma((16,)), dma((28,)), dma((52,)), dma((20,)), dma((12,)), dma((4,)),
            dma((2, 32)), dma((2, 8)), dma((4, 8)), dma((2, 32)), dma((2, 8)), dma((4, 4)), dma((4,)),
        ],
        compiler_params=pltpu.CompilerParams(
            collective_id=0, has_side_effects=True, vmem_limit_bytes=56 * 2**20),
    )(weight, grad, left, right, tokens)
    return pl.pallas_call(
        place,
        out_shape=(jax.ShapeDtypeStruct((256, 512), F32), jax.ShapeDtypeStruct((128, 512), BF)),
        in_specs=[any_] * 2,
        out_specs=(any_, any_),
        scratch_shapes=[pltpu.VMEM((256, 512), F32), pltpu.VMEM((128, 512), BF), dma((10,))],
    )(new_weight, output)


def solution(mesh):
    return jax.shard_map(
        shards,
        mesh=mesh,
        in_specs=(
            P("row", "col"),
            P("row", "col"),
            P("row", "col"),
            P("row", "col"),
            P("row", None),
        ),
        out_specs=(P("row", "col"), P("row", "col")),
        check_vma=False,
    )
```
